32 devices in a mesh: groups: 2 (over y), lon: 16 (over z, x, core).
Axes of the slice: x: 2, y: 2, z: 4, core: 2. Of those that a mesh axis runs over, the one named last changes fastest.
Arguments:
- ident_maps: bfloat16 [16, 128, 128, 128], P('groups', 'lon'), parts along dimension 0, may hold values from -6 to 6
- identity: int32 [4], P('groups'), parts along dimension 0, may hold values from 0 to 7
- audio: float32 [128, 256], P('groups'), parts along dimension 0, may hold values from -6 to 6
- audio_index: int32 [4], P('groups'), parts along dimension 0, may hold values from 0 to 63
- film_w: float32 [2, 256, 256], replicated, may hold values from -0.1875 to 0.1875
- conv_w: bfloat16 [2, 3, 3, 128, 128], replicated, may hold values from -0.1875 to 0.1875
- dout: bfloat16 [4, 128, 128, 128], P('groups', 'lon'), parts along dimension 0, may hold values from -18 to 18
Outputs:
- decoded: bfloat16 [4, 128, 128, 128], P('groups', 'lon'), parts along dimension 0
- conv_grad: float32 [4, 3, 3, 128, 128], P('groups'), parts along dimension 0
- film_grad: float32 [4, 256, 256], P('groups'), parts along dimension 0
The draws below stay inside these ranges and needn't reach their ends.
There are 2 independent parts, one for each index of `groups`. The reference program is written for one: setup_inputs(seed, part) draws one part's arguments, and reference() takes and returns one part's arrays. A program takes and returns all parts, laid end to end along the dimension named above; an argument that names none is the same for every part. Nothing has to cross between parts.
All inputs are finite; a program needn't handle non-finite values.
Results may differ from the reference program's by a relative error of at most 0.0052.
Values may be sent and summed in bfloat16 or wider, within the bound.
No kernel may reach another device: no remote copies, remote signals or barrier semaphores. Data moves between devices by JAX's collectives and lax.ppermute only.
A program may use at most 64 MiB of HBM per device.

```python
import math
import jax
import jax.numpy as jnp
from jax import lax

FRAMES = 2
ROWS = 128
C = 128
AD = 256
NID = 8
NA = 64
LAYERS = 2
NW = 128


def draw_dout(key, part):
    key_noise = jax.random.fold_in(key, 0)
    noise_draw = jnp.clip(jax.random.normal(key_noise, (FRAMES, NW, ROWS, C), jnp.float32), -6.0, 6.0)
    col_ramp = 1.0 + 2.0 * jnp.arange(NW, dtype=jnp.float32) / max(NW - 1, 1)
    col_ramp = col_ramp[None, :, None, None]
    values = noise_draw * col_ramp
    return values.astype(jnp.bfloat16)


def level_of(own_key, dims, shards, low, largest):
    factor_of = 1.0
    for position, shards_of in shards:
        steps = jax.random.uniform(jax.random.fold_in(jax.random.fold_in(own_key, 6), position), (shards_of,), jnp.float32, low / len(shards), largest / len(shards))
        factor_of = factor_of * jnp.repeat(jnp.exp(steps), dims[position] // shards_of).reshape((-1,) + (1,) * (len(dims) - 1 - position))
    return factor_of


def bell_draw(own_key, extent, deviation, limit, shards=(), kind=jnp.bfloat16):
    values = deviation * jax.random.normal(own_key, extent, jnp.float32)
    if shards:
        values = values * level_of(own_key, extent, shards, -0.22, 0.18)
    return jnp.clip(values, -limit, limit).astype(kind)


def setup_inputs(seed: int = 0, part: int = 0) -> dict:
    key_of = jax.random.split(jax.random.key(seed), 8)
    part_keys = jax.random.split(jax.random.fold_in(key_of[7], part), 8)
    return {
        "ident_maps": bell_draw(part_keys[0], (NID, NW, ROWS, C), 1.0, 6.0, ((1, 16),)),
        "identity": jax.random.randint(part_keys[1], (FRAMES,), 0, NID).astype(jnp.int32),
        "audio": bell_draw(part_keys[2], (NA, AD), 1.0, 6.0, (), jnp.float32),
        "audio_index": jax.random.randint(part_keys[3], (FRAMES,), 0, NA).astype(jnp.int32),
        "film_w": bell_draw(key_of[4], (LAYERS, AD, 2 * C), (4 * AD) ** -0.5, 0.1875, (), jnp.float32),
        "conv_w": bell_draw(key_of[5], (LAYERS, 3, 3, C, C), (9 * C) ** -0.5, 0.1875),
        "dout": draw_dout(jax.random.fold_in(jax.random.fold_in(key_of[7], part), 71), part),
    }


def conv_taps(padded, weight):
    frames, columns, rows, channels = padded.shape
    out_cols = columns - 2
    zero_row = jnp.zeros((frames, columns, 1, channels), padded.dtype)
    padded_rows = jnp.concatenate([zero_row, padded, zero_row], axis=2)
    stacked = jnp.concatenate([padded_rows[:, :, 0:rows], padded_rows[:, :, 1:rows + 1], padded_rows[:, :, 2:rows + 2]], axis=3)
    summed = jnp.zeros((frames * out_cols * rows, weight.shape[2]), jnp.float32)
    for offset in range(3):
        window = stacked[:, offset:offset + out_cols].reshape(-1, 3 * channels)
        summed = summed + jnp.dot(window, weight[offset], preferred_element_type=jnp.float32)
    return (summed.reshape(frames, out_cols, rows, weight.shape[2]), stacked)

def tap_grads(stacked, grad_pre, columns):
    flat_grad = grad_pre.reshape(-1, grad_pre.shape[-1])
    pieces = []
    for offset in range(3):
        window = stacked[:, offset:offset + columns].reshape(-1, stacked.shape[-1])
        pieces.append(lax.dot_general(window, flat_grad, (((0,), (0,)), ((), ())), preferred_element_type=jnp.float32))
    return jnp.stack(pieces)

def flip_taps(layer_w):
    channels = layer_w.shape[2]
    return layer_w[::-1, ::-1].swapaxes(2, 3).reshape(3, 3 * channels, channels)

def wrap_pad(field, depth):
    return jnp.concatenate([field[:, -depth:], field, field[:, :depth]], axis=1)

def reference(ident_maps, identity, audio, audio_index, film_w, conv_w, dout):
    weights = conv_w.reshape(LAYERS, 3, 3 * C, C)
    flips = [flip_taps(conv_w[layer]) for layer in range(LAYERS)]
    factor = 1.0 / math.sqrt(FRAMES * NW * ROWS)
    audio_rows = audio[audio_index]
    film_rows = jnp.einsum('fa,lak->lfk', audio_rows, film_w, precision=lax.Precision.HIGHEST)
    frame_films = jnp.transpose(film_rows, (1, 0, 2))

    def one_frame(accum, inputs):
        frame_id, frame_grad, frame_film, frame_audio = inputs
        conv_acc, film_acc = accum
        current = ident_maps[frame_id][None]
        saved_stack, saved_pre, saved_mod = ([], [], [])
        for layer in range(LAYERS):
            pre_act, stacked = conv_taps(wrap_pad(current, 1), weights[layer])
            gain = 1.0 + frame_film[layer, None, None, None, :C]
            modulated = pre_act * gain + frame_film[layer, None, None, None, C:]
            saved_stack.append(stacked)
            saved_pre.append(pre_act)
            saved_mod.append(modulated)
            current = jax.nn.silu(modulated).astype(jnp.bfloat16)
        grad_h = frame_grad[None].astype(jnp.float32) * factor
        wgrads = [None] * LAYERS
        stats = [None] * LAYERS
        for layer in reversed(range(LAYERS)):
            modulated = saved_mod[layer]
            gate_sig = jax.nn.sigmoid(modulated)
            grad_mod = grad_h * (gate_sig * (1.0 + modulated * (1.0 - gate_sig)))
            gain = 1.0 + frame_film[layer, None, None, None, :C]
            grad_pre = (grad_mod * gain).astype(jnp.bfloat16)
            stats[layer] = jnp.concatenate([lax.optimization_barrier(jnp.sum(grad_mod * saved_pre[layer], axis=(1, 2))), lax.optimization_barrier(jnp.sum(grad_mod, axis=(1, 2)))], axis=-1)[0]
            wgrads[layer] = tap_grads(saved_stack[layer], grad_pre, NW)
            if layer > 0:
                grad_h, unused = conv_taps(wrap_pad(grad_pre, 1), flips[layer])
        conv_acc = conv_acc + jnp.stack(wgrads)
        film_acc = film_acc + frame_audio[None, :, None] * jnp.stack(stats)[:, None, :]
        return ((conv_acc, film_acc), current[0])
    init = (jnp.zeros((LAYERS, 3, 3 * C, C), jnp.float32), jnp.zeros((LAYERS, AD, 2 * C), jnp.float32))
    (conv_acc, film_acc), decoded = lax.scan(one_frame, init, (identity, dout, frame_films, audio_rows))
    return (decoded, conv_acc.reshape(LAYERS, 3, 3, C, C), film_acc)
```

```python
import functools
import math

import jax
import jax.numpy as jnp
from jax import lax
from jax.experimental import pallas as pl
from jax.experimental.pallas import tpu as pltpu
from jax.sharding import PartitionSpec as P

AXIS = "lon"
RIM = 3
F32 = jnp.float32
BF16 = jnp.bfloat16


def chunk_of(count, largest):
    return max(size for size in range(1, largest + 1) if count % size == 0)


def shift_stack(values, rows):
    total = values.shape[0]
    place = lax.broadcasted_iota(jnp.int32, values.shape, 0) % rows
    above = jnp.where(place == 0, 0.0, pltpu.roll(values, 1, 0))
    below = jnp.where(place == rows - 1, 0.0, pltpu.roll(values, total - 1, 0))
    return jnp.concatenate([above.astype(BF16), values.astype(BF16), below.astype(BF16)], axis=1)


def windows(stack, frame, starts, size):
    parts = []
    for a in range(3):
        blocks = [stack[frame, start + a : start + a + size] for start in starts]
        blocks = [block.reshape(-1, block.shape[-1]) for block in blocks]
        parts.append(blocks[0] if len(blocks) == 1 else jnp.concatenate(blocks, axis=0))
    return jnp.concatenate(parts, axis=1)


def step_kernel(
    factor,
    identity,
    maps,
    low,
    high,
    dout,
    dlow,
    dhigh,
    film,
    weights,
    decoded,
    taps_0,
    taps_1,
    stats,
    first,
    stack_0,
    stack_1,
    stack_d,
    saved_pre,
    turned,
    sems,
):
    frames, columns, rows, channels = dout.shape
    copies = []
    for f in range(frames):
        copies.append(pltpu.make_async_copy(maps.at[identity[f]], first.at[f], sems.at[f]))
        copies[-1].start()

    def put(stack, f, start, size, values):
        stacked = shift_stack(values, rows)
        stack[f, start : start + size] = stacked.reshape(size, rows, 3 * channels)

    def flat(values):
        return values.reshape(-1, channels)

    def gain_of(layer, f):
        return 1.0 + film[layer, f : f + 1, :channels]

    def offset_of(layer, f):
        return film[layer, f : f + 1, channels:]

    for f in range(frames):
        put(stack_0, f, 0, RIM, flat(low[f].astype(F32)))
        put(stack_0, f, RIM + columns, RIM, flat(high[f].astype(F32)))
    inner = chunk_of(columns, 4)
    for f in range(frames):
        copies[f].wait()
        for c in range(0, columns, inner):
            put(stack_0, f, RIM + c, inner, flat(first[f, c : c + inner].astype(F32)))

    weight_0 = weights[0].reshape(9 * channels, channels)
    weight_1 = weights[1].reshape(9 * channels, channels)

    for f in range(frames):
        gain, offset = gain_of(0, f), offset_of(0, f)

        def forward_0(starts, size):
            pre = jnp.dot(windows(stack_0, f, starts, size), weight_0, preferred_element_type=F32)
            mod = pre * gain + offset
            return pre, mod * jax.nn.sigmoid(mod)

        pre, hidden = forward_0((1 - 1, columns + 2), 2)
        put(stack_1, f, 0, 2, hidden[: 2 * rows])
        put(stack_1, f, columns + 2, 2, hidden[2 * rows :])
        for c in range(0, columns, inner):
            pre, hidden = forward_0((c + 2,), inner)
            saved_pre[f, c : c + inner] = pre.reshape(inner, rows, channels)
            put(stack_1, f, c + 2, inner, hidden)

    sums = {}

    def collect(layer, f, grad_mod, pre):
        product = jnp.sum(grad_mod * pre, axis=0, keepdims=True)
        plain = jnp.sum(grad_mod, axis=0, keepdims=True)
        if (layer, f) in sums:
            before = sums[layer, f]
            sums[layer, f] = (before[0] + product, before[1] + plain)
        else:
            sums[layer, f] = (product, plain)

    for f in range(frames):
        gain, offset = gain_of(1, f), offset_of(1, f)

        def both_1(starts, size, grad):
            pre = jnp.dot(windows(stack_1, f, starts, size), weight_1, preferred_element_type=F32)
            mod = pre * gain + offset
            gate = jax.nn.sigmoid(mod)
            grad_mod = (grad.astype(F32) * factor) * (gate * (1.0 + mod * (1.0 - gate)))
            return pre, mod * gate, grad_mod, grad_mod * gain

        grad = jnp.concatenate([flat(dlow[f]), flat(dhigh[f])], axis=0)
        pre, hidden, grad_mod, grad_pre = both_1((0, columns + 1), 1, grad)
        put(stack_d, f, 0, 1, grad_pre[:rows])
        put(stack_d, f, columns + 1, 1, grad_pre[rows:])
        for c in range(0, columns, inner):
            pre, hidden, grad_mod, grad_pre = both_1((c + 1,), inner, flat(dout[f, c : c + inner]))
            decoded[f, c : c + inner] = hidden.astype(BF16).reshape(inner, rows, channels)
            collect(1, f, grad_mod, pre)
            put(stack_d, f, c + 1, inner, grad_pre)
            turned[f, :, c * rows : (c + inner) * rows] = grad_pre.T.astype(BF16)

    def tap_sums(stack, offset, out):
        for a in range(3):
            total = jnp.zeros((channels, 3 * channels), F32)
            for f in range(frames):
                window = stack[f, offset + a : offset + a + columns].reshape(-1, 3 * channels)
                total = total + jnp.dot(turned[f], window, preferred_element_type=F32)
            out[a * 3 * channels : (a + 1) * 3 * channels, :] = total.T.astype(out.dtype)

    tap_sums(stack_1, 1, taps_1)

    flipped = jnp.concatenate(
        [weights[1, 2 - a, 2 - b] for a in range(3) for b in range(3)], axis=1
    )
    for f in range(frames):
        gain, offset = gain_of(0, f), offset_of(0, f)
        for c in range(0, columns, inner):
            grad = lax.dot_general(
                windows(stack_d, f, (c,), inner),
                flipped,
                (((1,), (1,)), ((), ())),
                preferred_element_type=F32,
            )
            pre = flat(saved_pre[f, c : c + inner])
            mod = pre * gain + offset
            gate = jax.nn.sigmoid(mod)
            grad_mod = grad * (gate * (1.0 + mod * (1.0 - gate)))
            collect(0, f, grad_mod, pre)
            turned[f, :, c * rows : (c + inner) * rows] = (grad_mod * gain).T.astype(BF16)
    tap_sums(stack_0, 2, taps_0)

    for (layer, f), (product, plain) in sums.items():
        stats[layer, f : f + 1, :channels] = product
        stats[layer, f : f + 1, channels:] = plain


def local_step(factor, identity, maps, low, high, dout, dlow, dhigh, film, weights):
    frames, columns, rows, channels = dout.shape
    layers = weights.shape[0]
    vmem = pl.BlockSpec(memory_space=pltpu.VMEM)
    taps = jax.ShapeDtypeStruct((9 * channels, channels), BF16)
    return pl.pallas_call(
        functools.partial(step_kernel, factor),
        out_shape=(
            jax.ShapeDtypeStruct(dout.shape, BF16),
            taps,
            taps,
            jax.ShapeDtypeStruct((layers, frames, 2 * channels), F32),
        ),
        in_specs=[
            pl.BlockSpec(memory_space=pltpu.SMEM),
            pl.BlockSpec(memory_space=pl.ANY),
        ]
        + [vmem] * 7,
        out_specs=(vmem,) * 4,
        scratch_shapes=[
            pltpu.VMEM((frames, columns, rows, channels), BF16),
            pltpu.VMEM((frames, columns + 6, rows, 3 * channels), BF16),
            pltpu.VMEM((frames, columns + 4, rows, 3 * channels), BF16),
            pltpu.VMEM((frames, columns + 2, rows, 3 * channels), BF16),
            pltpu.VMEM((frames, columns, rows, channels), F32),
            pltpu.VMEM((frames, channels, columns * rows), BF16),
            pltpu.SemaphoreType.DMA((frames,)),
        ],
        compiler_params=pltpu.CompilerParams(vmem_limit_bytes=48 << 20),
        cost_estimate=pl.CostEstimate(
            flops=6 * 2 * 9 * channels * channels * frames * columns * rows,
            transcendentals=4 * frames * columns * rows * channels,
            bytes_accessed=8 << 20,
        ),
        name="decoder_step",
    )(identity, maps, low, high, dout, dlow, dhigh, film, weights)


def swap(value, bit):
    count = lax.axis_size(AXIS)
    return lax.ppermute(value, AXIS, [(i, i ^ bit) for i in range(count)])


def halve(value, bit):
    half = value.shape[0] // 2
    mine = (lax.axis_index(AXIS) // bit) % 2
    keep = lax.dynamic_slice_in_dim(value, mine * half, half, 0)
    send = lax.dynamic_slice_in_dim(value, (1 - mine) * half, half, 0)
    return (keep.astype(F32) + swap(send, bit).astype(F32)).astype(value.dtype)


def share(value, bit):
    return (value.astype(F32) + swap(value, bit).astype(F32)).astype(value.dtype)


def join(value, bit):
    other = swap(value, bit)
    mine = (lax.axis_index(AXIS) // bit) % 2
    return jnp.concatenate(
        [jnp.where(mine == 0, value, other), jnp.where(mine == 0, other, value)], axis=0
    )


def all_sums(first, second, small):
    bits = []
    while (1 << len(bits)) < lax.axis_size(AXIS):
        bits.append(1 << len(bits))
    orders = [list(bits), list(bits)]
    if len(bits) > 2:
        orders[1][1], orders[1][2] = bits[2], bits[1]
    values = [first, second]
    for step in range(len(bits)):
        for s in range(2):
            values[s] = (halve if step < 2 else share)(values[s], orders[s][step])
        small = share(small, orders[1][step])
    for step in reversed(range(min(2, len(bits)))):
        for s in range(2):
            values[s] = join(values[s], orders[s][step])
    return values[0], values[1], small


def local(ident_maps, identity, audio, audio_index, film_w, conv_w, dout):
    frames = identity.shape[0]
    layers = conv_w.shape[0]
    channels = conv_w.shape[3]
    columns, rows = ident_maps.shape[1:3]
    count = lax.axis_size(AXIS)
    factor = 1.0 / math.sqrt(frames * columns * count * rows)

    def edge(start):
        size = (1, RIM, rows, channels)
        return jnp.concatenate(
            [lax.dynamic_slice(ident_maps, (identity[f], start, 0, 0), size) for f in range(frames)]
        )

    forward = [(i, (i + 1) % count) for i in range(count)]
    backward = [(i, (i - 1) % count) for i in range(count)]
    low = lax.ppermute(edge(columns - RIM), AXIS, forward)
    high = lax.ppermute(edge(0), AXIS, backward)
    dlow = lax.ppermute(dout[:, columns - 1 :], AXIS, forward)
    dhigh = lax.ppermute(dout[:, :1], AXIS, backward)
    audio_rows = jnp.concatenate(
        [lax.dynamic_slice_in_dim(audio, audio_index[f], 1, 0) for f in range(frames)]
    )
    film = jnp.einsum("fa,lak->lfk", audio_rows, film_w, precision=lax.Precision.HIGHEST)
    decoded, taps_0, taps_1, stats = local_step(
        factor, identity, ident_maps, low, high, dout, dlow, dhigh, film, conv_w
    )
    sum_1, sum_0, stats = all_sums(taps_1, taps_0, stats)
    film_grad = jnp.einsum("fa,lfk->lak", audio_rows, stats, precision=lax.Precision.HIGHEST)
    conv_grad = jnp.stack([sum_0, sum_1]).astype(F32).reshape(layers, 3, 3, channels, channels)
    return decoded, conv_grad, film_grad


def solution(mesh):
    return jax.shard_map(
        local,
        mesh=mesh,
        in_specs=(
            P("groups", "lon", None, None),
            P("groups"),
            P("groups", None),
            P("groups"),
            P(),
            P(),
            P("groups", "lon", None, None),
        ),
        out_specs=(
            P("groups", "lon", None, None),
            P("groups", None, None, None, None),
            P("groups", None, None),
        ),
        check_vma=False,
    )
```

```python
import functools
import math

import jax
import jax.numpy as jnp
from jax import lax
from jax.experimental import pallas as pl
from jax.experimental.pallas import tpu as pltpu
from jax.sharding import PartitionSpec as P

AXIS = "lon"
RIM = 3
F32 = jnp.float32
BF16 = jnp.bfloat16
VMEM = pl.BlockSpec(memory_space=pltpu.VMEM)
SMEM = pl.BlockSpec(memory_space=pltpu.SMEM)
HBM = pl.BlockSpec(memory_space=pltpu.HBM)
ANY = pl.BlockSpec(memory_space=pl.ANY)


def parts_of(items, size):
    items = list(items)
    return [items[i : i + size] for i in range(0, len(items), size)]


def flat(values):
    return values.reshape(-1, values.shape[-1])


def shift_stack(values, rows):
    total = values.shape[0]
    place = lax.broadcasted_iota(jnp.int32, values.shape, 0) % rows
    above = jnp.where(place == 0, 0.0, pltpu.roll(values, 1, 0))
    below = jnp.where(place == rows - 1, 0.0, pltpu.roll(values, total - 1, 0))
    return jnp.concatenate([above.astype(BF16), values.astype(BF16), below.astype(BF16)], axis=1)


class Columns:
    def __init__(self, *pieces):
        self.place = {}
        for ref, columns in pieces:
            for i, column in enumerate(columns):
                self.place[column] = (ref, i)

    def get(self, f, column):
        ref, i = self.place[column]
        return ref[f, i]

    def put(self, f, columns, values, rows):
        for n, column in enumerate(columns):
            ref, i = self.place[column]
            ref[f, i] = values[n * rows : (n + 1) * rows]

    def rows_of(self, f, columns):
        blocks = [self.get(f, column) for column in columns]
        return blocks[0] if len(blocks) == 1 else jnp.concatenate(blocks, axis=0)

    def windows(self, f, columns):
        return jnp.concatenate(
            [self.rows_of(f, [column + a - 1 for column in columns]) for a in range(3)], axis=1
        )


def film_of(film, layer, f):
    channels = film.shape[2] // 2
    return 1.0 + film[layer, f : f + 1, :channels], film[layer, f : f + 1, channels:]


def forward_0(film, weights, h_0, h_1, pre_0, f, columns, rows):
    gain, offset = film_of(film, 0, f)
    weight = weights[0].reshape(-1, weights.shape[-1])
    pre = jnp.dot(h_0.windows(f, columns), weight, preferred_element_type=F32)
    mod = pre * gain + offset
    h_1.put(f, columns, shift_stack(mod * jax.nn.sigmoid(mod), rows), rows)
    for n, column in enumerate(columns):
        if column in pre_0.place:
            pre_0.put(f, [column], pre[n * rows : (n + 1) * rows], rows)


def both_1(factor, film, weights, h_1, dout, decoded, d_1, f, columns, rows):
    gain, offset = film_of(film, 1, f)
    weight = weights[1].reshape(-1, weights.shape[-1])
    pre = jnp.dot(h_1.windows(f, columns), weight, preferred_element_type=F32)
    mod = pre * gain + offset
    gate = jax.nn.sigmoid(mod)
    hidden = (mod * gate).astype(BF16)
    for n, column in enumerate(columns):
        if column in decoded.place:
            decoded.put(f, [column], hidden[n * rows : (n + 1) * rows], rows)
    grad = dout.rows_of(f, columns).astype(F32) * factor
    grad_mod = grad * (gate * (1.0 + mod * (1.0 - gate)))
    grad_pre = grad_mod * gain
    d_1.put(f, columns, shift_stack(grad_pre, rows), rows)
    return grad_pre, grad_mod, pre


def back_0(film, weights, d_1, pre_0, f, columns):
    gain, offset = film_of(film, 0, f)
    flipped = jnp.concatenate(
        [weights[1, 2 - a, 2 - b] for a in range(3) for b in range(3)], axis=1
    )
    grad = lax.dot_general(
        d_1.windows(f, columns), flipped, (((1,), (1,)), ((), ())), preferred_element_type=F32
    )
    pre = pre_0.rows_of(f, columns)
    mod = pre * gain + offset
    gate = jax.nn.sigmoid(mod)
    grad_mod = grad * (gate * (1.0 + mod * (1.0 - gate)))
    return grad_mod * gain, grad_mod, pre


class Sums:
    def __init__(self):
        self.stats = {}
        self.turned = []

    def add(self, f, columns, rows, grad_pre, grad_mod, pre):
        product = jnp.sum(grad_mod * pre, axis=0, keepdims=True)
        plain = jnp.sum(grad_mod, axis=0, keepdims=True)
        if f in self.stats:
            before = self.stats[f]
            self.stats[f] = (before[0] + product, before[1] + plain)
        else:
            self.stats[f] = (product, plain)
        self.turned.append((f, columns, grad_pre.T.astype(BF16)))

    def taps(self, field, a):
        total = None
        for f, columns, turned in self.turned:
            window = field.rows_of(f, [column + a - 1 for column in columns])
            term = jnp.dot(turned, window, preferred_element_type=F32)
            total = term if total is None else total + term
        return total

    def rows_of_stats(self):
        return jnp.concatenate([row for f in sorted(self.stats) for row in self.stats[f]], axis=0)


def put_message(mine, totals, stats, whole, keep, send):
    size = totals[0].shape[1]
    half = 3 * size // 2
    for a in range(3):
        whole[a * size : (a + 1) * size, :] = totals[a].T
    low, high = whole[:half, :], whole[half:, :]
    keep[:half, :] = jnp.where(mine == 0, low, high)
    send[:half, :] = jnp.where(mine == 0, high, low)
    tail = keep.shape[0] - half
    padded = jnp.concatenate([stats, jnp.zeros((tail - stats.shape[0], stats.shape[1]), F32)], axis=0)
    keep[half:, :] = padded
    send[half:, :] = padded


def edge_kernel(identity, maps, dout, outer, inner, sems):
    frames, columns = dout.shape[:2]
    mine = lax.rem(lax.axis_index(AXIS), 2)
    copies = []
    for side, out in enumerate((outer, inner)):
        at_end = mine if side == 0 else 1 - mine
        for f in range(frames):
            source = maps.at[identity[f], pl.ds(at_end * (columns - RIM), RIM)]
            copies.append(
                pltpu.make_async_copy(source, out.at[f, pl.ds(0, RIM)], sems.at[side, f, 0])
            )
            source = dout.at[f, pl.ds(at_end * (columns - 1), 1)]
            copies.append(
                pltpu.make_async_copy(source, out.at[f, pl.ds(RIM, 1)], sems.at[side, f, 1])
            )
    for copy in copies:
        copy.start()
    for copy in copies:
        copy.wait()


def inner_kernel(
    factor,
    identity,
    audio_index,
    maps,
    audio,
    film_w,
    weights,
    dout,
    film,
    audio_rows,
    stack_0,
    stack_1,
    stack_d,
    pre_0,
    decoded,
    taps_0,
    taps_1,
    stats,
    first,
    sems,
):
    frames, columns, rows = first.shape[:3]
    copies = []
    for f in range(frames):
        copies.append(pltpu.make_async_copy(maps.at[identity[f]], first.at[f], sems.at[f]))
    for copy in copies:
        copy.start()
    for f in range(frames):
        audio_rows[f : f + 1, :] = audio[pl.ds(audio_index[f], 1), :]
    for layer in range(film.shape[0]):
        film[layer] = jnp.dot(
            audio_rows[...],
            film_w[layer],
            precision=lax.Precision.HIGHEST,
            preferred_element_type=F32,
        )

    h_0 = Columns((stack_0, range(columns)))
    h_1 = Columns((stack_1, range(1, columns - 1)))
    d_1 = Columns((stack_d, range(2, columns - 2)))
    saved = Columns((pre_0, range(1, columns - 1)))
    out = Columns((decoded, range(2, columns - 2)))
    grads = Columns((dout, range(columns)))

    for f in range(frames):
        copies[f].wait()
        for some in parts_of(range(columns), 4):
            values = flat(first[f, some[0] : some[-1] + 1]).astype(F32)
            h_0.put(f, some, shift_stack(values, rows), rows)

    for f in range(frames):
        for some in parts_of(range(1, columns - 1), 3):
            forward_0(film, weights, h_0, h_1, saved, f, some, rows)
    sums_1, sums_0 = Sums(), Sums()
    for f in range(frames):
        some = list(range(2, columns - 2))
        sums_1.add(
            f, some, rows, *both_1(factor, film, weights, h_1, grads, out, d_1, f, some, rows)
        )
    for f in range(frames):
        some = list(range(3, columns - 3))
        sums_0.add(f, some, rows, *back_0(film, weights, d_1, saved, f, some))
    for a in range(3):
        taps_1[a] = sums_1.taps(h_1, a)
        taps_0[a] = sums_0.taps(h_0, a)
    stats[0] = sums_0.rows_of_stats()
    stats[1] = sums_1.rows_of_stats()


def rim_kernel(
    factor,
    outer,
    inner,
    dout,
    weights,
    film,
    stack_0,
    stack_1,
    decoded_a,
    taps_a,
    stats_a,
    decoded,
    rim_0,
    rim_d,
    rim_pre,
    keep,
    send,
    rim_1,
    hidden,
    whole,
    sems,
):
    frames, columns, rows = dout.shape[:3]
    mine = lax.rem(lax.axis_index(AXIS), 2)
    done = pltpu.make_async_copy(decoded_a, decoded.at[:, pl.ds(2, columns - 4)], sems.at[0])
    done.start()
    last = columns - 1
    h_0 = Columns(
        (stack_0, range(columns)), (rim_0, [-3, -2, -1, last + 1, last + 2, last + 3])
    )
    h_1 = Columns(
        (stack_1, range(1, last)), (rim_1, [-2, -1, 0, last, last + 1, last + 2])
    )
    d_1 = Columns((rim_d, [-1, 0, 1, last - 1, last, last + 1]))
    saved = Columns((rim_pre, [0, last]))
    out = Columns((hidden, [0, 1, last - 1, last]))
    grads = Columns((dout, range(columns)))

    def received(f, item, high):
        side = mine if high else 1 - mine
        return jnp.where(side == 0, inner[f, item].astype(F32), outer[f, item].astype(F32))

    class Edges(Columns):
        def get(self, f, column):
            if column in (-1, columns):
                return received(f, RIM, column == columns).astype(BF16)
            return grads.get(f, column)

    for f in range(frames):
        for n in range(RIM):
            low = received(f, n, False)
            h_0.put(f, [n - RIM], shift_stack(low, rows), rows)
            high = received(f, n, True)
            h_0.put(f, [columns + n], shift_stack(high, rows), rows)
    for f in range(frames):
        for some in ([-2, -1, 0], [last, last + 1, last + 2]):
            forward_0(film, weights, h_0, h_1, saved, f, some, rows)
    sums = Sums()
    edges = Edges()
    for f in range(frames):
        both_1(factor, film, weights, h_1, edges, out, d_1, f, [-1, last + 1], rows)
        some = [0, 1, last - 1, last]
        sums.add(f, some, rows, *both_1(factor, film, weights, h_1, edges, out, d_1, f, some, rows))
    ends = [
        pltpu.make_async_copy(
            hidden.at[:, pl.ds(0, 2)], decoded.at[:, pl.ds(0, 2)], sems.at[1]
        ),
        pltpu.make_async_copy(
            hidden.at[:, pl.ds(2, 2)], decoded.at[:, pl.ds(columns - 2, 2)], sems.at[2]
        ),
    ]
    for copy in ends:
        copy.start()
    totals = [taps_a[a] + sums.taps(h_1, a) for a in range(3)]
    put_message(mine, totals, stats_a[1] + sums.rows_of_stats(), whole, keep, send)
    done.wait()
    for copy in ends:
        copy.wait()


def back_kernel(
    weights,
    film,
    stack_0,
    rim_0,
    stack_d,
    rim_d,
    pre_0,
    rim_pre,
    taps_a,
    stats_a,
    keep,
    send,
    whole,
):
    frames, columns, rows = stack_0.shape[:3]
    mine = lax.rem(lax.axis_index(AXIS), 2)
    last = columns - 1
    h_0 = Columns(
        (stack_0, range(columns)), (rim_0, [-3, -2, -1, last + 1, last + 2, last + 3])
    )
    d_1 = Columns(
        (stack_d, range(2, columns - 2)), (rim_d, [-1, 0, 1, last - 1, last, last + 1])
    )
    saved = Columns((pre_0, range(1, last)), (rim_pre, [0, last]))
    sums = Sums()
    for f in range(frames):
        some = [0, 1, 2, last - 2, last - 1, last]
        sums.add(f, some, rows, *back_0(film, weights, d_1, saved, f, some))
    totals = [taps_a[a] + sums.taps(h_0, a) for a in range(3)]
    put_message(mine, totals, stats_a[0] + sums.rows_of_stats(), whole, keep, send)


def call(kernel, name, ins, outs, args, scratch=(), flops=0, out_specs=None, room=36):
    return pl.pallas_call(
        kernel,
        out_shape=tuple(jax.ShapeDtypeStruct(shape, dtype) for shape, dtype in outs),
        in_specs=ins,
        out_specs=tuple(out_specs) if out_specs else (VMEM,) * len(outs),
        scratch_shapes=list(scratch),
        compiler_params=pltpu.CompilerParams(vmem_limit_bytes=room << 20),
        cost_estimate=pl.CostEstimate(flops=flops, transcendentals=0, bytes_accessed=4 << 20),
        name=name,
    )(*args)


def swap(value, bit):
    count = lax.axis_size(AXIS)
    return lax.ppermute(value, AXIS, [(i, i ^ bit) for i in range(count)])


def mine_of(bit):
    return (lax.axis_index(AXIS) // bit) % 2


def rounded(value):
    return lax.reduce_precision(value, 8, 7)


def exchange(taps, stats, bit, split):
    high = rounded(stats)
    low = rounded(stats - high)
    if split:
        half = taps.shape[0] // 2
        mine = mine_of(bit)
        keep = lax.dynamic_slice_in_dim(taps, mine * half, half, 0)
        send = lax.dynamic_slice_in_dim(taps, (1 - mine) * half, half, 0)
    else:
        keep = send = rounded(taps)
    message = jnp.concatenate([send.astype(BF16), high.astype(BF16), low.astype(BF16)], axis=0)
    other = swap(message, bit).astype(F32)
    size, tail = send.shape[0], stats.shape[0]
    stats = (high + low) + (other[size : size + tail] + other[size + tail :])
    return keep + other[:size], stats


def join(value, bit):
    other = swap(value, bit)
    mine = mine_of(bit)
    return jnp.concatenate(
        [jnp.where(mine == 0, value, other), jnp.where(mine == 0, other, value)], axis=0
    )


def all_sums(messages, half):
    bits = []
    while (2 << len(bits)) < lax.axis_size(AXIS):
        bits.append(2 << len(bits))
    orders = [list(bits), list(bits)]
    if len(bits) > 1:
        orders[1][0], orders[1][1] = bits[1], bits[0]
    if len(bits) > 2:
        orders[0][1], orders[0][2] = bits[2], bits[1]
    state = []
    for keep, send in messages:
        total = keep + swap(send, 1)
        state.append((total[:half], total[half:]))
    for step in range(len(bits)):
        for s in range(2):
            state[s] = exchange(*state[s], orders[s][step], step == 0)
    taps = [value.astype(BF16) for value, _ in state]
    if bits:
        taps = [join(taps[s], orders[s][0]) for s in range(2)]
    taps = [join(value, 1) for value in taps]
    return taps, [stats for _, stats in state]


def local(ident_maps, identity, audio, audio_index, film_w, conv_w, dout):
    frames, columns, rows, channels = dout.shape
    layers = conv_w.shape[0]
    width = film_w.shape[1]
    count = lax.axis_size(AXIS)
    factor = 1.0 / math.sqrt(frames * columns * count * rows)
    unit = 2 * 9 * channels * channels * frames * rows

    edges = ((frames, RIM + 1, rows, channels), BF16)
    outer, inner = call(
        edge_kernel,
        "edges",
        [SMEM, HBM, HBM],
        [edges, edges],
        (identity, ident_maps, dout),
        [pltpu.SemaphoreType.DMA((2, frames, 2))],
        room=57,
    )
    pairs = [(i, (i + 1) % count if i % 2 else (i - 1) % count) for i in range(count)]
    outer = lax.ppermute(outer, AXIS, pairs)
    inner = swap(inner, 1)

    def stack(n):
        return ((frames, n, rows, 3 * channels), BF16)

    taps = ((3, channels, 3 * channels), F32)
    stats = ((layers, 2 * frames, channels), F32)
    (
        film,
        audio_rows,
        stack_0,
        stack_1,
        stack_d,
        pre_0,
        decoded_a,
        taps_0,
        taps_1,
        stats_a,
    ) = call(
        functools.partial(inner_kernel, factor),
        "inner_columns",
        [SMEM, SMEM, HBM] + [VMEM] * 4,
        [
            ((layers, frames, 2 * channels), F32),
            ((frames, width), F32),
            stack(columns),
            stack(columns - 2),
            stack(columns - 4),
            ((frames, columns - 2, rows, channels), F32),
            ((frames, columns - 4, rows, channels), BF16),
            taps,
            taps,
            stats,
        ],
        (identity, audio_index, ident_maps, audio, film_w, conv_w, dout),
        [
            pltpu.VMEM((frames, columns, rows, channels), BF16),
            pltpu.SemaphoreType.DMA((frames,)),
        ],
        18 * unit,
        room=46,
    )
    half = 9 * channels // 2
    message = ((half + 8, channels), F32)
    whole = pltpu.VMEM((9 * channels, channels), F32)
    decoded, rim_0, rim_d, rim_pre, keep_1, send_1 = call(
        functools.partial(rim_kernel, factor),
        "rim_columns",
        [VMEM] * 10,
        [
            (dout.shape, BF16),
            stack(6),
            stack(6),
            ((frames, 2, rows, channels), F32),
            message,
            message,
        ],
        (outer, inner, dout, conv_w, film, stack_0, stack_1, decoded_a, taps_1, stats_a),
        [
            pltpu.VMEM(stack(6)[0], BF16),
            pltpu.VMEM((frames, 4, rows, channels), BF16),
            whole,
            pltpu.SemaphoreType.DMA((3,)),
        ],
        16 * unit,
        [HBM] + [VMEM] * 5,
    )
    keep_0, send_0 = call(
        back_kernel,
        "back_columns",
        [VMEM] * 10,
        [message, message],
        (conv_w, film, stack_0, rim_0, stack_d, rim_d, pre_0, rim_pre, taps_0, stats_a),
        [whole],
        12 * unit,
    )
    (sum_1, sum_0), (stats_1, stats_0) = all_sums([(keep_1, send_1), (keep_0, send_0)], half)
    totals = jnp.stack([stats_0, stats_1])[:, : 2 * frames].reshape(layers, frames, 1, 2 * channels)
    film_grad = jnp.sum(audio_rows[None, :, :, None] * totals, axis=1)
    conv_grad = jnp.stack([sum_0, sum_1]).astype(F32).reshape(layers, 3, 3, channels, channels)
    return decoded, conv_grad, film_grad


def solution(mesh):
    return jax.shard_map(
        local,
        mesh=mesh,
        in_specs=(
            P("groups", "lon", None, None),
            P("groups"),
            P("groups", None),
            P("groups"),
            P(),
            P(),
            P("groups", "lon", None, None),
        ),
        out_specs=(
            P("groups", "lon", None, None),
            P("groups", None, None, None, None),
            P("groups", None, None),
        ),
        check_vma=False,
    )
```

```python
import functools
import math

import jax
import jax.numpy as jnp
from jax import lax
from jax.experimental import pallas as pl
from jax.experimental.pallas import tpu as pltpu
from jax.sharding import PartitionSpec as P

AXIS = "lon"
RIM = 3
F32 = jnp.float32
BF16 = jnp.bfloat16
VMEM = pl.BlockSpec(memory_space=pltpu.VMEM)
SMEM = pl.BlockSpec(memory_space=pltpu.SMEM)
HBM = pl.BlockSpec(memory_space=pltpu.HBM)
ANY = pl.BlockSpec(memory_space=pl.ANY)


def parts_of(items, size):
    items = list(items)
    return [items[i : i + size] for i in range(0, len(items), size)]


def flat(values):
    return values.reshape(-1, values.shape[-1])


def shift_stack(values, rows):
    total = values.shape[0]
    place = lax.broadcasted_iota(jnp.int32, values.shape, 0) % rows
    above = jnp.where(place == 0, 0.0, pltpu.roll(values, 1, 0))
    below = jnp.where(place == rows - 1, 0.0, pltpu.roll(values, total - 1, 0))
    return jnp.concatenate([above.astype(BF16), values.astype(BF16), below.astype(BF16)], axis=1)


class Columns:
    def __init__(self, *pieces):
        self.place = {}
        for ref, columns in pieces:
            for i, column in enumerate(columns):
                self.place[column] = (ref, i)

    def get(self, f, column):
        ref, i = self.place[column]
        return ref[f, i]

    def put(self, f, columns, values, rows):
        for n, column in enumerate(columns):
            ref, i = self.place[column]
            ref[f, i] = values[n * rows : (n + 1) * rows]

    def rows_of(self, f, columns):
        blocks = [self.get(f, column) for column in columns]
        return blocks[0] if len(blocks) == 1 else jnp.concatenate(blocks, axis=0)

    def windows(self, f, columns):
        return jnp.concatenate(
            [self.rows_of(f, [column + a - 1 for column in columns]) for a in range(3)], axis=1
        )


def film_of(film, layer, f):
    channels = film.shape[2] // 2
    return 1.0 + film[layer, f : f + 1, :channels], film[layer, f : f + 1, channels:]


def forward_0(film, weights, h_0, h_1, pre_0, f, columns, rows):
    gain, offset = film_of(film, 0, f)
    weight = weights[0].reshape(-1, weights.shape[-1])
    pre = jnp.dot(h_0.windows(f, columns), weight, preferred_element_type=F32)
    mod = pre * gain + offset
    h_1.put(f, columns, shift_stack(mod * jax.nn.sigmoid(mod), rows), rows)
    for n, column in enumerate(columns):
        if column in pre_0.place:
            pre_0.put(f, [column], pre[n * rows : (n + 1) * rows], rows)


def both_1(factor, film, weights, h_1, dout, decoded, d_1, f, columns, rows):
    gain, offset = film_of(film, 1, f)
    weight = weights[1].reshape(-1, weights.shape[-1])
    pre = jnp.dot(h_1.windows(f, columns), weight, preferred_element_type=F32)
    mod = pre * gain + offset
    gate = jax.nn.sigmoid(mod)
    hidden = (mod * gate).astype(BF16)
    for n, column in enumerate(columns):
        if column in decoded.place:
            decoded.put(f, [column], hidden[n * rows : (n + 1) * rows], rows)
    grad = dout.rows_of(f, columns).astype(F32) * factor
    grad_mod = grad * (gate * (1.0 + mod * (1.0 - gate)))
    grad_pre = grad_mod * gain
    d_1.put(f, columns, shift_stack(grad_pre, rows), rows)
    return grad_pre, grad_mod, pre


def back_0(film, weights, d_1, pre_0, f, columns):
    gain, offset = film_of(film, 0, f)
    flipped = jnp.concatenate(
        [weights[1, 2 - a, 2 - b] for a in range(3) for b in range(3)], axis=1
    )
    grad = lax.dot_general(
        d_1.windows(f, columns), flipped, (((1,), (1,)), ((), ())), preferred_element_type=F32
    )
    pre = pre_0.rows_of(f, columns)
    mod = pre * gain + offset
    gate = jax.nn.sigmoid(mod)
    grad_mod = grad * (gate * (1.0 + mod * (1.0 - gate)))
    return grad_mod * gain, grad_mod, pre


class Sums:
    def __init__(self):
        self.stats = {}
        self.turned = []

    def add(self, f, columns, rows, grad_pre, grad_mod, pre):
        product = jnp.sum(grad_mod * pre, axis=0, keepdims=True)
        plain = jnp.sum(grad_mod, axis=0, keepdims=True)
        if f in self.stats:
            before = self.stats[f]
            self.stats[f] = (before[0] + product, before[1] + plain)
        else:
            self.stats[f] = (product, plain)
        self.turned.append((f, columns, grad_pre.T.astype(BF16)))

    def taps(self, field, a):
        total = None
        for f, columns, turned in self.turned:
            window = field.rows_of(f, [column + a - 1 for column in columns])
            term = jnp.dot(turned, window, preferred_element_type=F32)
            total = term if total is None else total + term
        return total

    def rows_of_stats(self):
        return jnp.concatenate([row for f in sorted(self.stats) for row in self.stats[f]], axis=0)


def put_message(mine, totals, stats, whole, keep, send):
    size = totals[0].shape[1]
    half = 3 * size // 2
    for a in range(3):
        whole[a * size : (a + 1) * size, :] = totals[a].T
    low, high = whole[:half, :], whole[half:, :]
    keep[:half, :] = jnp.where(mine == 0, low, high)
    send[:half, :] = jnp.where(mine == 0, high, low)
    tail = keep.shape[0] - half
    padded = jnp.concatenate([stats, jnp.zeros((tail - stats.shape[0], stats.shape[1]), F32)], axis=0)
    keep[half:, :] = padded
    send[half:, :] = padded


def edge_kernel(identity, maps, dout, outer, inner, sems):
    frames, columns = dout.shape[:2]
    mine = lax.rem(lax.axis_index(AXIS), 2)
    copies = []
    for side, out in enumerate((outer, inner)):
        at_end = mine if side == 0 else 1 - mine
        for f in range(frames):
            source = maps.at[identity[f], pl.ds(at_end * (columns - RIM), RIM)]
            copies.append(
                pltpu.make_async_copy(source, out.at[f, pl.ds(0, RIM)], sems.at[side, f, 0])
            )
            source = dout.at[f, pl.ds(at_end * (columns - 1), 1)]
            copies.append(
                pltpu.make_async_copy(source, out.at[f, pl.ds(RIM, 1)], sems.at[side, f, 1])
            )
    for copy in copies:
        copy.start()
    for copy in copies:
        copy.wait()


def inner_kernel(
    factor,
    identity,
    audio_index,
    maps,
    audio,
    film_w,
    weights,
    dout,
    film,
    audio_rows,
    stack_0,
    stack_1,
    stack_d,
    pre_0,
    decoded,
    taps_0,
    taps_1,
    stats,
    first,
    sems,
):
    frames, columns, rows = first.shape[:3]
    copies = []
    for f in range(frames):
        copies.append(pltpu.make_async_copy(maps.at[identity[f]], first.at[f], sems.at[f]))
    for copy in copies:
        copy.start()
    for f in range(frames):
        audio_rows[f : f + 1, :] = audio[pl.ds(audio_index[f], 1), :]
    for layer in range(film.shape[0]):
        film[layer] = jnp.dot(
            audio_rows[...],
            film_w[layer],
            precision=lax.Precision.HIGHEST,
            preferred_element_type=F32,
        )

    h_0 = Columns((stack_0, range(columns)))
    h_1 = Columns((stack_1, range(1, columns - 1)))
    d_1 = Columns((stack_d, range(2, columns - 2)))
    saved = Columns((pre_0, range(1, columns - 1)))
    out = Columns((decoded, range(2, columns - 2)))
    grads = Columns((dout, range(columns)))

    for f in range(frames):
        copies[f].wait()
        for some in parts_of(range(columns), 4):
            values = flat(first[f, some[0] : some[-1] + 1]).astype(F32)
            h_0.put(f, some, shift_stack(values, rows), rows)

    for f in range(frames):
        for some in parts_of(range(1, columns - 1), 6):
            forward_0(film, weights, h_0, h_1, saved, f, some, rows)
    sums_1, sums_0 = Sums(), Sums()
    for f in range(frames):
        some = list(range(2, columns - 2))
        sums_1.add(
            f, some, rows, *both_1(factor, film, weights, h_1, grads, out, d_1, f, some, rows)
        )
    for f in range(frames):
        some = list(range(3, columns - 3))
        sums_0.add(f, some, rows, *back_0(film, weights, d_1, saved, f, some))
    for a in range(3):
        taps_1[a] = sums_1.taps(h_1, a)
        taps_0[a] = sums_0.taps(h_0, a)
    stats[0] = sums_0.rows_of_stats()
    stats[1] = sums_1.rows_of_stats()


def rim_kernel(
    factor,
    outer,
    inner,
    dout,
    weights,
    film,
    stack_0,
    stack_1,
    stack_d,
    pre_0,
    decoded_a,
    taps_0,
    taps_1,
    stats_a,
    decoded,
    keep_1,
    send_1,
    keep_0,
    send_0,
    rim_0,
    rim_1,
    rim_d,
    rim_pre,
    hidden,
    whole,
    sems,
):
    frames, columns, rows = dout.shape[:3]
    mine = lax.rem(lax.axis_index(AXIS), 2)
    done = pltpu.make_async_copy(decoded_a, decoded.at[:, pl.ds(2, columns - 4)], sems.at[0])
    done.start()
    last = columns - 1
    h_0 = Columns(
        (stack_0, range(columns)), (rim_0, [-3, -2, -1, last + 1, last + 2, last + 3])
    )
    h_1 = Columns(
        (stack_1, range(1, last)), (rim_1, [-2, -1, 0, last, last + 1, last + 2])
    )
    d_1 = Columns(
        (stack_d, range(2, columns - 2)), (rim_d, [-1, 0, 1, last - 1, last, last + 1])
    )
    saved = Columns((pre_0, range(1, last)), (rim_pre, [0, last]))
    out = Columns((hidden, [0, 1, last - 1, last]))
    grads = Columns((dout, range(columns)))

    def received(f, item, high):
        side = mine if high else 1 - mine
        return jnp.where(side == 0, inner[f, item].astype(F32), outer[f, item].astype(F32))

    class Edges(Columns):
        def get(self, f, column):
            if column in (-1, columns):
                return received(f, RIM, column == columns).astype(BF16)
            return grads.get(f, column)

    for f in range(frames):
        for n in range(RIM):
            low = received(f, n, False)
            h_0.put(f, [n - RIM], shift_stack(low, rows), rows)
            high = received(f, n, True)
            h_0.put(f, [columns + n], shift_stack(high, rows), rows)
    for f in range(frames):
        for some in ([-2, -1, 0, last, last + 1, last + 2],):
            forward_0(film, weights, h_0, h_1, saved, f, some, rows)
    sums_0, sums_1 = Sums(), Sums()
    edges = Edges()
    for f in range(frames):
        both_1(factor, film, weights, h_1, edges, out, d_1, f, [-1, last + 1], rows)
        some = [0, 1, last - 1, last]
        sums_1.add(
            f, some, rows, *both_1(factor, film, weights, h_1, edges, out, d_1, f, some, rows)
        )
    ends = [
        pltpu.make_async_copy(
            hidden.at[:, pl.ds(0, 2)], decoded.at[:, pl.ds(0, 2)], sems.at[1]
        ),
        pltpu.make_async_copy(
            hidden.at[:, pl.ds(2, 2)], decoded.at[:, pl.ds(columns - 2, 2)], sems.at[2]
        ),
    ]
    for copy in ends:
        copy.start()
    for f in range(frames):
        some = [0, 1, 2, last - 2, last - 1, last]
        sums_0.add(f, some, rows, *back_0(film, weights, d_1, saved, f, some))
    totals = [taps_1[a] + sums_1.taps(h_1, a) for a in range(3)]
    put_message(mine, totals, stats_a[1] + sums_1.rows_of_stats(), whole, keep_1, send_1)
    totals = [taps_0[a] + sums_0.taps(h_0, a) for a in range(3)]
    put_message(mine, totals, stats_a[0] + sums_0.rows_of_stats(), whole, keep_0, send_0)
    done.wait()
    for copy in ends:
        copy.wait()


def call(kernel, name, ins, outs, args, scratch=(), flops=0, out_specs=None, room=36):
    return pl.pallas_call(
        kernel,
        out_shape=tuple(jax.ShapeDtypeStruct(shape, dtype) for shape, dtype in outs),
        in_specs=ins,
        out_specs=tuple(out_specs) if out_specs else (VMEM,) * len(outs),
        scratch_shapes=list(scratch),
        compiler_params=pltpu.CompilerParams(vmem_limit_bytes=room << 20),
        cost_estimate=pl.CostEstimate(flops=flops, transcendentals=0, bytes_accessed=4 << 20),
        name=name,
    )(*args)


def swap(value, bits):
    count = lax.axis_size(AXIS)
    return lax.ppermute(value, AXIS, [(i, i ^ bits[i % 2]) for i in range(count)])


def mine_of(bits):
    place = lax.axis_index(AXIS)
    if bits[0] == bits[1]:
        return (place // bits[0]) % 2
    return jnp.where(place % 2 == 0, (place // bits[0]) % 2, (place // bits[1]) % 2)


def rounded(value):
    return lax.reduce_precision(value, 8, 7)


def exchange(taps, stats, bit, split):
    high = rounded(stats)
    low = rounded(stats - high)
    if split:
        half = taps.shape[0] // 2
        mine = mine_of(bit)
        keep = lax.dynamic_slice_in_dim(taps, mine * half, half, 0)
        send = lax.dynamic_slice_in_dim(taps, (1 - mine) * half, half, 0)
    else:
        keep = send = rounded(taps)
    message = jnp.concatenate([send.astype(BF16), high.astype(BF16), low.astype(BF16)], axis=0)
    other = swap(message, bit).astype(F32)
    size, tail = send.shape[0], stats.shape[0]
    stats = (high + low) + (other[size : size + tail] + other[size + tail :])
    return keep + other[:size], stats


def join(value, bit):
    other = swap(value, bit)
    mine = mine_of(bit)
    return jnp.concatenate(
        [jnp.where(mine == 0, value, other), jnp.where(mine == 0, other, value)], axis=0
    )


def all_sums(messages, half):
    bits = []
    while (2 << len(bits)) < lax.axis_size(AXIS):
        bits.append(2 << len(bits))
    one = bits[:1] + bits[2:] + bits[1:2]
    other = bits[1:2] + bits[:1] + bits[2:]
    orders = [list(zip(one, other)), list(zip(other, one))]
    state = []
    for keep, send in messages:
        total = keep + swap(send, (1, 1))
        state.append((total[:half], total[half:]))
    for step in range(len(bits)):
        for s in range(2):
            state[s] = exchange(*state[s], orders[s][step], step == 0)
    taps = [value.astype(BF16) for value, _ in state]
    if bits:
        taps = [join(taps[s], orders[s][0]) for s in range(2)]
    taps = [join(value, (1, 1)) for value in taps]
    return taps, [stats for _, stats in state]


def local(ident_maps, identity, audio, audio_index, film_w, conv_w, dout):
    frames, columns, rows, channels = dout.shape
    layers = conv_w.shape[0]
    width = film_w.shape[1]
    count = lax.axis_size(AXIS)
    factor = 1.0 / math.sqrt(frames * columns * count * rows)
    unit = 2 * 9 * channels * channels * frames * rows

    edges = ((frames, RIM + 1, rows, channels), BF16)
    outer, inner = call(
        edge_kernel,
        "edges",
        [SMEM, HBM, HBM],
        [edges, edges],
        (identity, ident_maps, dout),
        [pltpu.SemaphoreType.DMA((2, frames, 2))],
        room=53,
    )
    pairs = [(i, (i + 1) % count if i % 2 else (i - 1) % count) for i in range(count)]
    outer = lax.ppermute(outer, AXIS, pairs)
    inner = swap(inner, (1, 1))

    def stack(n):
        return ((frames, n, rows, 3 * channels), BF16)

    taps = ((3, channels, 3 * channels), F32)
    stats = ((layers, 2 * frames, channels), F32)
    (
        film,
        audio_rows,
        stack_0,
        stack_1,
        stack_d,
        pre_0,
        decoded_a,
        taps_0,
        taps_1,
        stats_a,
    ) = call(
        functools.partial(inner_kernel, factor),
        "inner_columns",
        [SMEM, SMEM, HBM] + [VMEM] * 4,
        [
            ((layers, frames, 2 * channels), F32),
            ((frames, width), F32),
            stack(columns),
            stack(columns - 2),
            stack(columns - 4),
            ((frames, columns - 2, rows, channels), F32),
            ((frames, columns - 4, rows, channels), BF16),
            taps,
            taps,
            stats,
        ],
        (identity, audio_index, ident_maps, audio, film_w, conv_w, dout),
        [
            pltpu.VMEM((frames, columns, rows, channels), BF16),
            pltpu.SemaphoreType.DMA((frames,)),
        ],
        18 * unit,
        room=46,
    )
    half = 9 * channels // 2
    message = ((half + 8, channels), F32)
    whole = pltpu.VMEM((9 * channels, channels), F32)
    decoded, keep_1, send_1, keep_0, send_0 = call(
        functools.partial(rim_kernel, factor),
        "rim_columns",
        [VMEM] * 13,
        [(dout.shape, BF16)] + [message] * 4,
        (outer, inner, dout, conv_w, film, stack_0, stack_1, stack_d, pre_0, decoded_a)
        + (taps_0, taps_1, stats_a),
        [
            pltpu.VMEM(stack(6)[0], BF16),
            pltpu.VMEM(stack(6)[0], BF16),
            pltpu.VMEM(stack(6)[0], BF16),
            pltpu.VMEM((frames, 2, rows, channels), F32),
            pltpu.VMEM((frames, 4, rows, channels), BF16),
            whole,
            pltpu.SemaphoreType.DMA((3,)),
        ],
        28 * unit,
        [HBM] + [VMEM] * 4,
    )
    (sum_0, sum_1), (stats_0, stats_1) = all_sums([(keep_0, send_0), (keep_1, send_1)], half)
    totals = jnp.stack([stats_0, stats_1])[:, : 2 * frames].reshape(layers, frames, 1, 2 * channels)
    film_grad = jnp.sum(audio_rows[None, :, :, None] * totals, axis=1)
    conv_grad = jnp.stack([sum_0, sum_1]).astype(F32).reshape(layers, 3, 3, channels, channels)
    return decoded, conv_grad, film_grad


def solution(mesh):
    return jax.shard_map(
        local,
        mesh=mesh,
        in_specs=(
            P("groups", "lon", None, None),
            P("groups"),
            P("groups", None),
            P("groups"),
            P(),
            P(),
            P("groups", "lon", None, None),
        ),
        out_specs=(
            P("groups", "lon", None, None),
            P("groups", None, None, None, None),
            P("groups", None, None),
        ),
        check_vma=False,
    )
```

```python
import functools
import math

import jax
import jax.numpy as jnp
from jax import lax
from jax.experimental import pallas as pl
from jax.experimental.pallas import tpu as pltpu
from jax.sharding import PartitionSpec as P

AXIS = "lon"
RIM = 3
F32 = jnp.float32
BF16 = jnp.bfloat16
VMEM = pl.BlockSpec(memory_space=pltpu.VMEM)
SMEM = pl.BlockSpec(memory_space=pltpu.SMEM)
HBM = pl.BlockSpec(memory_space=pltpu.HBM)
ANY = pl.BlockSpec(memory_space=pl.ANY)


def parts_of(items, size):
    items = list(items)
    return [items[i : i + size] for i in range(0, len(items), size)]


def flat(values):
    return values.reshape(-1, values.shape[-1])


def shift_stack(values, rows):
    total = values.shape[0]
    place = lax.broadcasted_iota(jnp.int32, values.shape, 0) % rows
    above = jnp.where(place == 0, 0.0, pltpu.roll(values, 1, 0))
    below = jnp.where(place == rows - 1, 0.0, pltpu.roll(values, total - 1, 0))
    return jnp.concatenate([above.astype(BF16), values.astype(BF16), below.astype(BF16)], axis=1)


class Columns:
    def __init__(self, *pieces):
        self.place = {}
        for ref, columns in pieces:
            for i, column in enumerate(columns):
                self.place[column] = (ref, i)

    def get(self, f, column):
        ref, i = self.place[column]
        return ref[f, i]

    def put(self, f, columns, values, rows):
        for n, column in enumerate(columns):
            ref, i = self.place[column]
            ref[f, i] = values[n * rows : (n + 1) * rows]

    def rows_of(self, f, columns):
        blocks = [self.get(f, column) for column in columns]
        return blocks[0] if len(blocks) == 1 else jnp.concatenate(blocks, axis=0)

    def windows(self, f, columns):
        return jnp.concatenate(
            [self.rows_of(f, [column + a - 1 for column in columns]) for a in range(3)], axis=1
        )


def film_of(film, layer, f):
    channels = film.shape[2] // 2
    return 1.0 + film[layer, f : f + 1, :channels], film[layer, f : f + 1, channels:]


def forward_0(film, weights, h_0, h_1, pre_0, f, columns, rows):
    gain, offset = film_of(film, 0, f)
    weight = weights[0].reshape(-1, weights.shape[-1])
    pre = jnp.dot(h_0.windows(f, columns), weight, preferred_element_type=F32)
    mod = pre * gain + offset
    h_1.put(f, columns, shift_stack(mod * jax.nn.sigmoid(mod), rows), rows)
    for n, column in enumerate(columns):
        if column in pre_0.place:
            pre_0.put(f, [column], pre[n * rows : (n + 1) * rows], rows)


def both_1(factor, film, weights, h_1, dout, decoded, d_1, f, columns, rows):
    gain, offset = film_of(film, 1, f)
    weight = weights[1].reshape(-1, weights.shape[-1])
    pre = jnp.dot(h_1.windows(f, columns), weight, preferred_element_type=F32)
    mod = pre * gain + offset
    gate = jax.nn.sigmoid(mod)
    hidden = (mod * gate).astype(BF16)
    for n, column in enumerate(columns):
        if column in decoded.place:
            decoded.put(f, [column], hidden[n * rows : (n + 1) * rows], rows)
    grad = dout.rows_of(f, columns).astype(F32) * factor
    grad_mod = grad * (gate * (1.0 + mod * (1.0 - gate)))
    grad_pre = grad_mod * gain
    d_1.put(f, columns, shift_stack(grad_pre, rows), rows)
    return grad_pre, grad_mod, pre


def back_0(film, weights, d_1, pre_0, f, columns):
    gain, offset = film_of(film, 0, f)
    flipped = jnp.concatenate(
        [weights[1, 2 - a, 2 - b] for a in range(3) for b in range(3)], axis=1
    )
    grad = lax.dot_general(
        d_1.windows(f, columns), flipped, (((1,), (1,)), ((), ())), preferred_element_type=F32
    )
    pre = pre_0.rows_of(f, columns)
    mod = pre * gain + offset
    gate = jax.nn.sigmoid(mod)
    grad_mod = grad * (gate * (1.0 + mod * (1.0 - gate)))
    return grad_mod * gain, grad_mod, pre


class Sums:
    def __init__(self):
        self.stats = {}
        self.turned = []

    def add(self, f, columns, rows, grad_pre, grad_mod, pre):
        product = jnp.sum(grad_mod * pre, axis=0, keepdims=True)
        plain = jnp.sum(grad_mod, axis=0, keepdims=True)
        if f in self.stats:
            before = self.stats[f]
            self.stats[f] = (before[0] + product, before[1] + plain)
        else:
            self.stats[f] = (product, plain)
        self.turned.append((f, columns, grad_pre.T.astype(BF16)))

    def taps(self, field, a):
        total = None
        for f, columns, turned in self.turned:
            window = field.rows_of(f, [column + a - 1 for column in columns])
            term = jnp.dot(turned, window, preferred_element_type=F32)
            total = term if total is None else total + term
        return total

    def rows_of_stats(self):
        return jnp.concatenate([row for f in sorted(self.stats) for row in self.stats[f]], axis=0)


def put_message(mine, totals, stats, whole, keep, send):
    size = totals[0].shape[1]
    half = 3 * size // 2
    for a in range(3):
        whole[a * size : (a + 1) * size, :] = totals[a].T
    low, high = whole[:half, :], whole[half:, :]
    keep[:half, :] = jnp.where(mine == 0, low, high)
    send[:half, :] = jnp.where(mine == 0, high, low).astype(BF16)
    tail = keep.shape[0] - half
    if tail > stats.shape[0]:
        blank = jnp.zeros((tail - stats.shape[0], stats.shape[1]), F32)
        stats = jnp.concatenate([stats, blank], axis=0)
    coarse = stats.astype(BF16)
    rest = (stats - coarse.astype(F32)).astype(BF16)
    keep[half:, :] = coarse.astype(F32) + rest.astype(F32)
    send[half:, :] = jnp.concatenate([coarse, rest], axis=0)


def edge_kernel(identity, maps, dout, outer, inner, sems):
    frames, columns = dout.shape[:2]
    mine = lax.rem(lax.axis_index(AXIS), 2)
    copies = []
    for side, out in enumerate((outer, inner)):
        at_end = mine if side == 0 else 1 - mine
        for f in range(frames):
            source = maps.at[identity[f], pl.ds(at_end * (columns - RIM), RIM)]
            copies.append(
                pltpu.make_async_copy(source, out.at[f, pl.ds(0, RIM)], sems.at[side, f, 0])
            )
            source = dout.at[f, pl.ds(at_end * (columns - 1), 1)]
            copies.append(
                pltpu.make_async_copy(source, out.at[f, pl.ds(RIM, 1)], sems.at[side, f, 1])
            )
    for copy in copies:
        copy.start()
    for copy in copies:
        copy.wait()


def inner_kernel(
    factor,
    identity,
    audio_index,
    maps,
    audio,
    film_w,
    weights,
    dout,
    film,
    audio_rows,
    stack_0,
    stack_1,
    stack_d,
    pre_0,
    decoded,
    taps_0,
    taps_1,
    stats,
    first,
    sems,
):
    frames, columns, rows = first.shape[:3]
    copies = []
    for f in range(frames):
        copies.append(pltpu.make_async_copy(maps.at[identity[f]], first.at[f], sems.at[f]))
    for copy in copies:
        copy.start()
    for f in range(frames):
        audio_rows[f : f + 1, :] = audio[pl.ds(audio_index[f], 1), :]
    for layer in range(film.shape[0]):
        film[layer] = jnp.dot(
            audio_rows[...],
            film_w[layer],
            precision=lax.Precision.HIGHEST,
            preferred_element_type=F32,
        )

    h_0 = Columns((stack_0, range(columns)))
    h_1 = Columns((stack_1, range(1, columns - 1)))
    d_1 = Columns((stack_d, range(2, columns - 2)))
    saved = Columns((pre_0, range(1, columns - 1)))
    out = Columns((decoded, range(2, columns - 2)))
    grads = Columns((dout, range(columns)))

    for f in range(frames):
        copies[f].wait()
        for some in parts_of(range(columns), 4):
            values = flat(first[f, some[0] : some[-1] + 1]).astype(F32)
            h_0.put(f, some, shift_stack(values, rows), rows)

    for f in range(frames):
        for some in parts_of(range(1, columns - 1), 6):
            forward_0(film, weights, h_0, h_1, saved, f, some, rows)
    sums_1, sums_0 = Sums(), Sums()
    for f in range(frames):
        some = list(range(2, columns - 2))
        sums_1.add(
            f, some, rows, *both_1(factor, film, weights, h_1, grads, out, d_1, f, some, rows)
        )
    for f in range(frames):
        some = list(range(3, columns - 3))
        sums_0.add(f, some, rows, *back_0(film, weights, d_1, saved, f, some))
    for a in range(3):
        taps_1[a] = sums_1.taps(h_1, a)
        taps_0[a] = sums_0.taps(h_0, a)
    stats[0] = sums_0.rows_of_stats()
    stats[1] = sums_1.rows_of_stats()


def rim_kernel(
    factor,
    outer,
    inner,
    dout,
    weights,
    film,
    stack_0,
    stack_1,
    stack_d,
    pre_0,
    decoded_a,
    taps_0,
    taps_1,
    stats_a,
    decoded,
    keep_1,
    send_1,
    keep_0,
    send_0,
    rim_0,
    rim_1,
    rim_d,
    rim_pre,
    hidden,
    whole,
    sems,
):
    frames, columns, rows = dout.shape[:3]
    mine = lax.rem(lax.axis_index(AXIS), 2)
    done = pltpu.make_async_copy(decoded_a, decoded.at[:, pl.ds(2, columns - 4)], sems.at[0])
    done.start()
    last = columns - 1
    h_0 = Columns(
        (stack_0, range(columns)), (rim_0, [-3, -2, -1, last + 1, last + 2, last + 3])
    )
    h_1 = Columns(
        (stack_1, range(1, last)), (rim_1, [-2, -1, 0, last, last + 1, last + 2])
    )
    d_1 = Columns(
        (stack_d, range(2, columns - 2)), (rim_d, [-1, 0, 1, last - 1, last, last + 1])
    )
    saved = Columns((pre_0, range(1, last)), (rim_pre, [0, last]))
    out = Columns((hidden, [0, 1, last - 1, last]))
    grads = Columns((dout, range(columns)))

    def received(f, item, high):
        side = mine if high else 1 - mine
        return jnp.where(side == 0, inner[f, item].astype(F32), outer[f, item].astype(F32))

    class Edges(Columns):
        def get(self, f, column):
            if column in (-1, columns):
                return received(f, RIM, column == columns).astype(BF16)
            return grads.get(f, column)

    for f in range(frames):
        for n in range(RIM):
            low = received(f, n, False)
            h_0.put(f, [n - RIM], shift_stack(low, rows), rows)
            high = received(f, n, True)
            h_0.put(f, [columns + n], shift_stack(high, rows), rows)
    for f in range(frames):
        for some in ([-2, -1, 0, last, last + 1, last + 2],):
            forward_0(film, weights, h_0, h_1, saved, f, some, rows)
    sums_0, sums_1 = Sums(), Sums()
    edges = Edges()
    for f in range(frames):
        both_1(factor, film, weights, h_1, edges, out, d_1, f, [-1, last + 1], rows)
        some = [0, 1, last - 1, last]
        sums_1.add(
            f, some, rows, *both_1(factor, film, weights, h_1, edges, out, d_1, f, some, rows)
        )
    ends = [
        pltpu.make_async_copy(
            hidden.at[:, pl.ds(0, 2)], decoded.at[:, pl.ds(0, 2)], sems.at[1]
        ),
        pltpu.make_async_copy(
            hidden.at[:, pl.ds(2, 2)], decoded.at[:, pl.ds(columns - 2, 2)], sems.at[2]
        ),
    ]
    for copy in ends:
        copy.start()
    for f in range(frames):
        some = [0, 1, 2, last - 2, last - 1, last]
        sums_0.add(f, some, rows, *back_0(film, weights, d_1, saved, f, some))
    totals = [taps_1[a] + sums_1.taps(h_1, a) for a in range(3)]
    put_message(mine, totals, stats_a[1] + sums_1.rows_of_stats(), whole, keep_1, send_1)
    totals = [taps_0[a] + sums_0.taps(h_0, a) for a in range(3)]
    put_message(mine, totals, stats_a[0] + sums_0.rows_of_stats(), whole, keep_0, send_0)
    done.wait()
    for copy in ends:
        copy.wait()


def call(kernel, name, ins, outs, args, scratch=(), flops=0, out_specs=None, room=36):
    return pl.pallas_call(
        kernel,
        out_shape=tuple(jax.ShapeDtypeStruct(shape, dtype) for shape, dtype in outs),
        in_specs=ins,
        out_specs=tuple(out_specs) if out_specs else (VMEM,) * len(outs),
        scratch_shapes=list(scratch),
        compiler_params=pltpu.CompilerParams(vmem_limit_bytes=room << 20),
        cost_estimate=pl.CostEstimate(flops=flops, transcendentals=0, bytes_accessed=4 << 20),
        name=name,
    )(*args)


def swap(value, bits):
    count = lax.axis_size(AXIS)
    return lax.ppermute(value, AXIS, [(i, i ^ bits[i % 2]) for i in range(count)])


def mine_of(bits):
    place = lax.axis_index(AXIS)
    if bits[0] == bits[1]:
        return (place // bits[0]) % 2
    return jnp.where(place % 2 == 0, (place // bits[0]) % 2, (place // bits[1]) % 2)


def rounded(value):
    return lax.reduce_precision(value, 8, 7)


def exchange(taps, stats, bit, split):
    high = rounded(stats)
    low = rounded(stats - high)
    if split:
        half = taps.shape[0] // 2
        mine = mine_of(bit)
        keep = lax.dynamic_slice_in_dim(taps, mine * half, half, 0)
        send = lax.dynamic_slice_in_dim(taps, (1 - mine) * half, half, 0)
    else:
        keep = send = rounded(taps)
    message = jnp.concatenate([send.astype(BF16), high.astype(BF16), low.astype(BF16)], axis=0)
    other = swap(message, bit).astype(F32)
    size, tail = send.shape[0], stats.shape[0]
    stats = (high + low) + (other[size : size + tail] + other[size + tail :])
    return keep + other[:size], stats


def join(value, bit):
    other = swap(value, bit)
    mine = mine_of(bit)
    return jnp.concatenate(
        [jnp.where(mine == 0, value, other), jnp.where(mine == 0, other, value)], axis=0
    )


def all_sums(messages, half):
    bits = []
    while (2 << len(bits)) < lax.axis_size(AXIS):
        bits.append(2 << len(bits))
    one = bits[:1] + bits[2:] + bits[1:2]
    other = bits[1:2] + bits[:1] + bits[2:]
    orders = [list(zip(one, other)), list(zip(other, one))]
    state = []
    for keep, send in messages:
        other = swap(send, (1, 1)).astype(F32)
        tail = keep.shape[0] - half
        stats = keep[half:] + (other[half : half + tail] + other[half + tail :])
        state.append((keep[:half] + other[:half], stats))
    for step in range(len(bits)):
        for s in range(2):
            state[s] = exchange(*state[s], orders[s][step], step == 0)
    taps = [value.astype(BF16) for value, _ in state]
    if bits:
        taps = [join(taps[s], orders[s][0]) for s in range(2)]
    taps = [join(value, (1, 1)) for value in taps]
    return taps, [stats for _, stats in state]


def local(ident_maps, identity, audio, audio_index, film_w, conv_w, dout):
    frames, columns, rows, channels = dout.shape
    layers = conv_w.shape[0]
    width = film_w.shape[1]
    count = lax.axis_size(AXIS)
    factor = 1.0 / math.sqrt(frames * columns * count * rows)
    unit = 2 * 9 * channels * channels * frames * rows

    edges = ((frames, RIM + 1, rows, channels), BF16)
    outer, inner = call(
        edge_kernel,
        "edges",
        [SMEM, HBM, HBM],
        [edges, edges],
        (identity, ident_maps, dout),
        [pltpu.SemaphoreType.DMA((2, frames, 2))],
        room=53,
    )
    pairs = [(i, (i + 1) % count if i % 2 else (i - 1) % count) for i in range(count)]
    outer = lax.ppermute(outer, AXIS, pairs)
    inner = swap(inner, (1, 1))

    def stack(n):
        return ((frames, n, rows, 3 * channels), BF16)

    taps = ((3, channels, 3 * channels), F32)
    stats = ((layers, 2 * frames, channels), F32)
    (
        film,
        audio_rows,
        stack_0,
        stack_1,
        stack_d,
        pre_0,
        decoded_a,
        taps_0,
        taps_1,
        stats_a,
    ) = call(
        functools.partial(inner_kernel, factor),
        "inner_columns",
        [SMEM, SMEM, HBM] + [VMEM] * 4,
        [
            ((layers, frames, 2 * channels), F32),
            ((frames, width), F32),
            stack(columns),
            stack(columns - 2),
            stack(columns - 4),
            ((frames, columns - 2, rows, channels), F32),
            ((frames, columns - 4, rows, channels), BF16),
            taps,
            taps,
            stats,
        ],
        (identity, audio_index, ident_maps, audio, film_w, conv_w, dout),
        [
            pltpu.VMEM((frames, columns, rows, channels), BF16),
            pltpu.SemaphoreType.DMA((frames,)),
        ],
        18 * unit,
        room=46,
    )
    half = 9 * channels // 2
    tail = (2 * frames + 7) // 8 * 8
    message = [((half + tail, channels), F32), ((half + 2 * tail, channels), BF16)]
    whole = pltpu.VMEM((9 * channels, channels), F32)
    decoded, keep_1, send_1, keep_0, send_0 = call(
        functools.partial(rim_kernel, factor),
        "rim_columns",
        [VMEM] * 13,
        [(dout.shape, BF16)] + message * 2,
        (outer, inner, dout, conv_w, film, stack_0, stack_1, stack_d, pre_0, decoded_a)
        + (taps_0, taps_1, stats_a),
        [
            pltpu.VMEM(stack(6)[0], BF16),
            pltpu.VMEM(stack(6)[0], BF16),
            pltpu.VMEM(stack(6)[0], BF16),
            pltpu.VMEM((frames, 2, rows, channels), F32),
            pltpu.VMEM((frames, 4, rows, channels), BF16),
            whole,
            pltpu.SemaphoreType.DMA((3,)),
        ],
        28 * unit,
        [HBM] + [VMEM] * 4,
    )
    (sum_0, sum_1), (stats_0, stats_1) = all_sums([(keep_0, send_0), (keep_1, send_1)], half)
    totals = jnp.stack([stats_0, stats_1])[:, : 2 * frames].reshape(layers, frames, 1, 2 * channels)
    film_grad = jnp.sum(audio_rows[None, :, :, None] * totals, axis=1)
    conv_grad = jnp.stack([sum_0, sum_1]).astype(F32).reshape(layers, 3, 3, channels, channels)
    return decoded, conv_grad, film_grad


def solution(mesh):
    return jax.shard_map(
        local,
        mesh=mesh,
        in_specs=(
            P("groups", "lon", None, None),
            P("groups"),
            P("groups", None),
            P("groups"),
            P(),
            P(),
            P("groups", "lon", None, None),
        ),
        out_specs=(
            P("groups", "lon", None, None),
            P("groups", None, None, None, None),
            P("groups", None, None),
        ),
        check_vma=False,
    )
```

```python
import functools
import math

import jax
import jax.numpy as jnp
from jax import lax
from jax.experimental import pallas as pl
from jax.experimental.pallas import tpu as pltpu
from jax.sharding import PartitionSpec as P

AXIS = "lon"
RIM = 3
F32 = jnp.float32
BF16 = jnp.bfloat16
VMEM = pl.BlockSpec(memory_space=pltpu.VMEM)
SMEM = pl.BlockSpec(memory_space=pltpu.SMEM)
HBM = pl.BlockSpec(memory_space=pltpu.HBM)
ANY = pl.BlockSpec(memory_space=pl.ANY)


def parts_of(items, size):
    items = list(items)
    return [items[i : i + size] for i in range(0, len(items), size)]


def flat(values):
    return values.reshape(-1, values.shape[-1])


def shift_stack(values, rows):
    total = values.shape[0]
    place = lax.broadcasted_iota(jnp.int32, values.shape, 0) % rows
    above = jnp.where(place == 0, 0.0, pltpu.roll(values, 1, 0))
    below = jnp.where(place == rows - 1, 0.0, pltpu.roll(values, total - 1, 0))
    return jnp.concatenate([above.astype(BF16), values.astype(BF16), below.astype(BF16)], axis=1)


class Columns:
    def __init__(self, *pieces):
        self.place = {}
        for ref, columns in pieces:
            for i, column in enumerate(columns):
                self.place[column] = (ref, i)

    def get(self, f, column):
        ref, i = self.place[column]
        return ref[f, i]

    def put(self, f, columns, values, rows):
        for n, column in enumerate(columns):
            ref, i = self.place[column]
            ref[f, i] = values[n * rows : (n + 1) * rows]

    def rows_of(self, f, columns):
        blocks = [self.get(f, column) for column in columns]
        return blocks[0] if len(blocks) == 1 else jnp.concatenate(blocks, axis=0)

    def windows(self, f, columns):
        return jnp.concatenate(
            [self.rows_of(f, [column + a - 1 for column in columns]) for a in range(3)], axis=1
        )


def film_of(film, layer, f):
    channels = film.shape[2] // 2
    return 1.0 + film[layer, f : f + 1, :channels], film[layer, f : f + 1, channels:]


def forward_0(film, weights, h_0, h_1, pre_0, f, columns, rows):
    gain, offset = film_of(film, 0, f)
    weight = weights[0].reshape(-1, weights.shape[-1])
    pre = jnp.dot(h_0.windows(f, columns), weight, preferred_element_type=F32)
    mod = pre * gain + offset
    h_1.put(f, columns, shift_stack(mod * jax.nn.sigmoid(mod), rows), rows)
    for n, column in enumerate(columns):
        if column in pre_0.place:
            pre_0.put(f, [column], pre[n * rows : (n + 1) * rows], rows)


def both_1(factor, film, weights, h_1, dout, decoded, d_1, f, columns, rows):
    gain, offset = film_of(film, 1, f)
    weight = weights[1].reshape(-1, weights.shape[-1])
    pre = jnp.dot(h_1.windows(f, columns), weight, preferred_element_type=F32)
    mod = pre * gain + offset
    gate = jax.nn.sigmoid(mod)
    hidden = (mod * gate).astype(BF16)
    for n, column in enumerate(columns):
        if column in decoded.place:
            decoded.put(f, [column], hidden[n * rows : (n + 1) * rows], rows)
    grad = dout.rows_of(f, columns).astype(F32) * factor
    grad_mod = grad * (gate * (1.0 + mod * (1.0 - gate)))
    grad_pre = grad_mod * gain
    d_1.put(f, columns, shift_stack(grad_pre, rows), rows)
    return grad_pre, grad_mod, pre


def back_0(film, weights, d_1, pre_0, f, columns):
    gain, offset = film_of(film, 0, f)
    flipped = jnp.concatenate(
        [weights[1, 2 - a, 2 - b] for a in range(3) for b in range(3)], axis=1
    )
    grad = lax.dot_general(
        d_1.windows(f, columns), flipped, (((1,), (1,)), ((), ())), preferred_element_type=F32
    )
    pre = pre_0.rows_of(f, columns)
    mod = pre * gain + offset
    gate = jax.nn.sigmoid(mod)
    grad_mod = grad * (gate * (1.0 + mod * (1.0 - gate)))
    return grad_mod * gain, grad_mod, pre


class Sums:
    def __init__(self):
        self.stats = {}
        self.turned = []

    def add(self, f, columns, rows, grad_pre, grad_mod, pre):
        product = jnp.sum(grad_mod * pre, axis=0, keepdims=True)
        plain = jnp.sum(grad_mod, axis=0, keepdims=True)
        if f in self.stats:
            before = self.stats[f]
            self.stats[f] = (before[0] + product, before[1] + plain)
        else:
            self.stats[f] = (product, plain)
        self.turned.append((f, columns, grad_pre.T.astype(BF16)))

    def taps(self, field, a):
        total = None
        for f, columns, turned in self.turned:
            window = field.rows_of(f, [column + a - 1 for column in columns])
            term = jnp.dot(turned, window, preferred_element_type=F32)
            total = term if total is None else total + term
        return total

    def rows_of_stats(self):
        return jnp.concatenate([row for f in sorted(self.stats) for row in self.stats[f]], axis=0)


def put_message(mine, totals, stats, whole, keep, send):
    size = totals[0].shape[1]
    half = 3 * size // 2
    for a in range(3):
        whole[a * size : (a + 1) * size, :] = totals[a].T
    low, high = whole[:half, :], whole[half:, :]
    keep[:half, :] = jnp.where(mine == 0, low, high)
    send[:half, :] = jnp.where(mine == 0, high, low).astype(BF16)
    tail = keep.shape[0] - half
    if tail > stats.shape[0]:
        blank = jnp.zeros((tail - stats.shape[0], stats.shape[1]), F32)
        stats = jnp.concatenate([stats, blank], axis=0)
    coarse = stats.astype(BF16)
    rest = (stats - coarse.astype(F32)).astype(BF16)
    keep[half:, :] = coarse.astype(F32) + rest.astype(F32)
    send[half:, :] = jnp.concatenate([coarse, rest], axis=0)


def edge_kernel(identity, maps, dout, outer, inner, sems):
    frames, columns = dout.shape[:2]
    mine = lax.rem(lax.axis_index(AXIS), 2)
    copies = []
    for side, out in enumerate((outer, inner)):
        at_end = mine if side == 0 else 1 - mine
        for f in range(frames):
            source = maps.at[identity[f], pl.ds(at_end * (columns - RIM), RIM)]
            copies.append(
                pltpu.make_async_copy(source, out.at[f, pl.ds(0, RIM)], sems.at[side, f, 0])
            )
            source = dout.at[f, pl.ds(at_end * (columns - 1), 1)]
            copies.append(
                pltpu.make_async_copy(source, out.at[f, pl.ds(RIM, 1)], sems.at[side, f, 1])
            )
    for copy in copies:
        copy.start()
    for copy in copies:
        copy.wait()


def inner_kernel(
    factor,
    identity,
    audio_index,
    maps,
    audio,
    film_w,
    weights,
    dout,
    film,
    audio_rows,
    stack_0,
    stack_1,
    stack_d,
    pre_0,
    decoded,
    taps_0,
    taps_1,
    stats,
    first,
    sems,
):
    frames, columns, rows = first.shape[:3]
    copies = []
    for f in range(frames):
        copies.append(pltpu.make_async_copy(maps.at[identity[f]], first.at[f], sems.at[f]))
    for copy in copies:
        copy.start()
    for f in range(frames):
        audio_rows[f : f + 1, :] = audio[pl.ds(audio_index[f], 1), :]
    for layer in range(film.shape[0]):
        film[layer] = jnp.dot(
            audio_rows[...],
            film_w[layer],
            precision=lax.Precision.HIGHEST,
            preferred_element_type=F32,
        )

    h_0 = Columns((stack_0, range(columns)))
    h_1 = Columns((stack_1, range(1, columns - 1)))
    d_1 = Columns((stack_d, range(2, columns - 2)))
    saved = Columns((pre_0, range(1, columns - 1)))
    out = Columns((decoded, range(2, columns - 2)))
    grads = Columns((dout, range(columns)))

    for f in range(frames):
        copies[f].wait()
        for some in parts_of(range(columns), 4):
            values = flat(first[f, some[0] : some[-1] + 1]).astype(F32)
            h_0.put(f, some, shift_stack(values, rows), rows)

    for f in range(frames):
        for some in parts_of(range(1, columns - 1), 6):
            forward_0(film, weights, h_0, h_1, saved, f, some, rows)
    sums_1, sums_0 = Sums(), Sums()
    for f in range(frames):
        some = list(range(2, columns - 2))
        sums_1.add(
            f, some, rows, *both_1(factor, film, weights, h_1, grads, out, d_1, f, some, rows)
        )
    for f in range(frames):
        some = list(range(3, columns - 3))
        sums_0.add(f, some, rows, *back_0(film, weights, d_1, saved, f, some))
    for a in range(3):
        taps_1[a] = sums_1.taps(h_1, a)
        taps_0[a] = sums_0.taps(h_0, a)
    stats[0] = sums_0.rows_of_stats()
    stats[1] = sums_1.rows_of_stats()


def rim_kernel(
    factor,
    outer,
    inner,
    dout,
    weights,
    film,
    stack_0,
    stack_1,
    stack_d,
    pre_0,
    decoded_a,
    taps_0,
    taps_1,
    stats_a,
    decoded,
    keep_1,
    send_1,
    keep_0,
    send_0,
    rim_0,
    rim_1,
    rim_d,
    rim_pre,
    hidden,
    whole,
    sems,
):
    frames, columns, rows = dout.shape[:3]
    mine = lax.rem(lax.axis_index(AXIS), 2)
    done = pltpu.make_async_copy(decoded_a, decoded.at[:, pl.ds(2, columns - 4)], sems.at[0])
    done.start()
    last = columns - 1
    h_0 = Columns(
        (stack_0, range(columns)), (rim_0, [-3, -2, -1, last + 1, last + 2, last + 3])
    )
    h_1 = Columns(
        (stack_1, range(1, last)), (rim_1, [-2, -1, 0, last, last + 1, last + 2])
    )
    d_1 = Columns(
        (stack_d, range(2, columns - 2)), (rim_d, [-1, 0, 1, last - 1, last, last + 1])
    )
    saved = Columns((pre_0, range(1, last)), (rim_pre, [0, last]))
    out = Columns((hidden, [0, 1, last - 1, last]))
    grads = Columns((dout, range(columns)))

    def received(f, item, high):
        side = mine if high else 1 - mine
        return jnp.where(side == 0, inner[f, item].astype(F32), outer[f, item].astype(F32))

    class Edges(Columns):
        def get(self, f, column):
            if column in (-1, columns):
                return received(f, RIM, column == columns).astype(BF16)
            return grads.get(f, column)

    for f in range(frames):
        for n in range(RIM):
            low = received(f, n, False)
            h_0.put(f, [n - RIM], shift_stack(low, rows), rows)
            high = received(f, n, True)
            h_0.put(f, [columns + n], shift_stack(high, rows), rows)
    for f in range(frames):
        for some in ([-2, -1, 0, last, last + 1, last + 2],):
            forward_0(film, weights, h_0, h_1, saved, f, some, rows)
    sums_0, sums_1 = Sums(), Sums()
    edges = Edges()
    for f in range(frames):
        some = [0, 1, last - 1, last]
        sums_1.add(
            f, some, rows, *both_1(factor, film, weights, h_1, edges, out, d_1, f, some, rows)
        )
    for f in range(frames):
        both_1(factor, film, weights, h_1, edges, out, d_1, f, [-1, last + 1], rows)
    ends = [
        pltpu.make_async_copy(
            hidden.at[:, pl.ds(0, 2)], decoded.at[:, pl.ds(0, 2)], sems.at[1]
        ),
        pltpu.make_async_copy(
            hidden.at[:, pl.ds(2, 2)], decoded.at[:, pl.ds(columns - 2, 2)], sems.at[2]
        ),
    ]
    for copy in ends:
        copy.start()
    for f in range(frames):
        some = [0, 1, 2, last - 2, last - 1, last]
        sums_0.add(f, some, rows, *back_0(film, weights, d_1, saved, f, some))
    totals = [taps_1[a] + sums_1.taps(h_1, a) for a in range(3)]
    put_message(mine, totals, stats_a[1] + sums_1.rows_of_stats(), whole, keep_1, send_1)
    totals = [taps_0[a] + sums_0.taps(h_0, a) for a in range(3)]
    put_message(mine, totals, stats_a[0] + sums_0.rows_of_stats(), whole, keep_0, send_0)
    done.wait()
    for copy in ends:
        copy.wait()


def call(kernel, name, ins, outs, args, scratch=(), flops=0, out_specs=None, room=36):
    return pl.pallas_call(
        kernel,
        out_shape=tuple(jax.ShapeDtypeStruct(shape, dtype) for shape, dtype in outs),
        in_specs=ins,
        out_specs=tuple(out_specs) if out_specs else (VMEM,) * len(outs),
        scratch_shapes=list(scratch),
        compiler_params=pltpu.CompilerParams(vmem_limit_bytes=room << 20),
        cost_estimate=pl.CostEstimate(flops=flops, transcendentals=0, bytes_accessed=4 << 20),
        name=name,
    )(*args)


def swap(value, bits):
    count = lax.axis_size(AXIS)
    return lax.ppermute(value, AXIS, [(i, i ^ bits[i % 2]) for i in range(count)])


def mine_of(bits):
    place = lax.axis_index(AXIS)
    if bits[0] == bits[1]:
        return (place // bits[0]) % 2
    return jnp.where(place % 2 == 0, (place // bits[0]) % 2, (place // bits[1]) % 2)


def rounded(value):
    return lax.reduce_precision(value, 8, 7)


def exchange(taps, stats, bit, split):
    high = rounded(stats)
    low = rounded(stats - high)
    if split:
        half = taps.shape[0] // 2
        mine = mine_of(bit)
        keep = lax.dynamic_slice_in_dim(taps, mine * half, half, 0)
        send = lax.dynamic_slice_in_dim(taps, (1 - mine) * half, half, 0)
    else:
        keep = send = rounded(taps)
    message = jnp.concatenate([send.astype(BF16), high.astype(BF16), low.astype(BF16)], axis=0)
    other = swap(message, bit).astype(F32)
    size, tail = send.shape[0], stats.shape[0]
    stats = (high + low) + (other[size : size + tail] + other[size + tail :])
    return keep + other[:size], stats


def join(value, bit):
    other = swap(value, bit)
    mine = mine_of(bit)
    return jnp.concatenate(
        [jnp.where(mine == 0, value, other), jnp.where(mine == 0, other, value)], axis=0
    )


def all_sums(messages, half):
    bits = []
    while (2 << len(bits)) < lax.axis_size(AXIS):
        bits.append(2 << len(bits))
    one = bits[:1] + bits[2:] + bits[1:2]
    other = bits[1:2] + bits[:1] + bits[2:]
    orders = [list(zip(one, other)), list(zip(other, one))]
    state = []
    for keep, send in messages:
        other = swap(send, (1, 1)).astype(F32)
        tail = keep.shape[0] - half
        stats = keep[half:] + (other[half : half + tail] + other[half + tail :])
        state.append((keep[:half] + other[:half], stats))
    for step in range(len(bits)):
        for s in range(2):
            state[s] = exchange(*state[s], orders[s][step], step == 0)
    taps = [value.astype(BF16) for value, _ in state]
    if bits:
        taps = [join(taps[s], orders[s][0]) for s in range(2)]
    taps = [join(value, (1, 1)) for value in taps]
    return taps, [stats for _, stats in state]


def local(ident_maps, identity, audio, audio_index, film_w, conv_w, dout):
    frames, columns, rows, channels = dout.shape
    layers = conv_w.shape[0]
    width = film_w.shape[1]
    count = lax.axis_size(AXIS)
    factor = 1.0 / math.sqrt(frames * columns * count * rows)
    unit = 2 * 9 * channels * channels * frames * rows

    edges = ((frames, RIM + 1, rows, channels), BF16)
    outer, inner = call(
        edge_kernel,
        "edges",
        [SMEM, HBM, HBM],
        [edges, edges],
        (identity, ident_maps, dout),
        [pltpu.SemaphoreType.DMA((2, frames, 2))],
        room=53,
    )
    pairs = [(i, (i + 1) % count if i % 2 else (i - 1) % count) for i in range(count)]
    outer = lax.ppermute(outer, AXIS, pairs)
    inner = swap(inner, (1, 1))

    def stack(n):
        return ((frames, n, rows, 3 * channels), BF16)

    taps = ((3, channels, 3 * channels), F32)
    stats = ((layers, 2 * frames, channels), F32)
    (
        film,
        audio_rows,
        stack_0,
        stack_1,
        stack_d,
        pre_0,
        decoded_a,
        taps_0,
        taps_1,
        stats_a,
    ) = call(
        functools.partial(inner_kernel, factor),
        "inner_columns",
        [SMEM, SMEM, HBM] + [VMEM] * 4,
        [
            ((layers, frames, 2 * channels), F32),
            ((frames, width), F32),
            stack(columns),
            stack(columns - 2),
            stack(columns - 4),
            ((frames, columns - 2, rows, channels), F32),
            ((frames, columns - 4, rows, channels), BF16),
            taps,
            taps,
            stats,
        ],
        (identity, audio_index, ident_maps, audio, film_w, conv_w, dout),
        [
            pltpu.VMEM((frames, columns, rows, channels), BF16),
            pltpu.SemaphoreType.DMA((frames,)),
        ],
        18 * unit,
        room=46,
    )
    half = 9 * channels // 2
    tail = (2 * frames + 7) // 8 * 8
    message = [((half + tail, channels), F32), ((half + 2 * tail, channels), BF16)]
    whole = pltpu.VMEM((9 * channels, channels), F32)
    decoded, keep_1, send_1, keep_0, send_0 = call(
        functools.partial(rim_kernel, factor),
        "rim_columns",
        [VMEM] * 13,
        [(dout.shape, BF16)] + message * 2,
        (outer, inner, dout, conv_w, film, stack_0, stack_1, stack_d, pre_0, decoded_a)
        + (taps_0, taps_1, stats_a),
        [
            pltpu.VMEM(stack(6)[0], BF16),
            pltpu.VMEM(stack(6)[0], BF16),
            pltpu.VMEM(stack(6)[0], BF16),
            pltpu.VMEM((frames, 2, rows, channels), F32),
            pltpu.VMEM((frames, 4, rows, channels), BF16),
            whole,
            pltpu.SemaphoreType.DMA((3,)),
        ],
        28 * unit,
        [HBM] + [VMEM] * 4,
    )
    (sum_0, sum_1), (stats_0, stats_1) = all_sums([(keep_0, send_0), (keep_1, send_1)], half)
    totals = jnp.stack([stats_0, stats_1])[:, : 2 * frames].reshape(layers, frames, 1, 2 * channels)
    film_grad = jnp.sum(audio_rows[None, :, :, None] * totals, axis=1)
    conv_grad = jnp.stack([sum_0, sum_1]).astype(F32).reshape(layers, 3, 3, channels, channels)
    return decoded, conv_grad, film_grad


def solution(mesh):
    return jax.shard_map(
        local,
        mesh=mesh,
        in_specs=(
            P("groups", "lon", None, None),
            P("groups"),
            P("groups", None),
            P("groups"),
            P(),
            P(),
            P("groups", "lon", None, None),
        ),
        out_specs=(
            P("groups", "lon", None, None),
            P("groups", None, None, None, None),
            P("groups", None, None),
        ),
        check_vma=False,
    )
```
